32 devices in a mesh: depth: 8 (over z, y), height: 4 (over x, core).
Axes of the slice: x: 2, y: 2, z: 4, core: 2. Of those that a mesh axis runs over, the one named last changes fastest.
Arguments:
- volume: float32 [8, 64, 2048], P('height', 'depth'), may hold values from -6 to 6
- measured: float32 [16, 8, 2048], P(None, 'height', 'depth'), may hold values from -12 to 12
- taps: float32 [4, 16, 64], P(None, None, 'depth'), may hold values from 0.01 to 0.1
- band_offset: int32 [16, 8], replicated, may hold values from -64 to 64
- angle_index: int32 [16], replicated, may hold values from 0 to 719
Outputs:
- denoised: float32 [8, 64, 2048], P('height', 'depth')
The draws below stay inside these ranges and needn't reach their ends.
Inputs may be any that keep to these rules, and one draw needn't show every extreme that they name: `band_offset`: band offsets of every angle and brick lie within plus or minus 64.
All inputs are finite; a program needn't handle non-finite values.
Results may differ from the reference program's by a relative error of at most 0.0003.
Values sent between devices are 32-bit elements; how exact they have to be, the bound alone decides.
No kernel may reach another device: no remote copies, remote signals or barrier semaphores. Data moves between devices by JAX's collectives and lax.ppermute only.
A program may use at most 64 MiB of HBM per device.

```python
import math
import jax
import jax.numpy as jnp
from jax import lax

NX = 2048
CD = 8
ANGLES = 16
TAPS = 4
OFFMAX = 64
N_VIEWS = 720
SWEEPS = 2
ND = 64
NH = 8
BRICKS = 8
N_DEPTH = 8


def touch_ends(result, stream_key, least, largest):
    index_at = [jax.random.randint(jax.random.fold_in(stream_key, axis), (), 0, length) for axis, length in enumerate(result.shape)]
    widest = result.shape.index(max(result.shape))
    beside = index_at[:widest] + [(index_at[widest] + 1) % result.shape[widest]] + index_at[widest + 1:]
    return result.at[tuple(index_at)].set(least).at[tuple(beside)].set(largest)


def levels(stream_key, shape, shards, smallest, top_value):
    def one(axis_at, shards_of):
        heights = jax.random.uniform(jax.random.fold_in(jax.random.fold_in(stream_key, 6), axis_at), (shards_of,), jnp.float32, smallest / len(shards), top_value / len(shards))
        return jnp.repeat(jnp.exp(heights), shape[axis_at] // shards_of).reshape((-1,) + (1,) * (len(shape) - axis_at - 1))

    gain = one(*shards[0])
    for cut in shards[1:]:
        gain = gain * one(*cut)
    return gain


def noise(stream_key, shape, scale, most, pieces=(), kind=jnp.bfloat16):
    drawn = scale * jax.random.normal(stream_key, shape, jnp.float32)
    if pieces:
        drawn = drawn * levels(stream_key, shape, pieces, -0.22, 0.18)
    return jnp.clip(drawn, -most, most).astype(kind)


def setup_inputs(seed: int = 0) -> dict:
    arg_keys = jax.random.split(jax.random.key(seed), 6)
    return {
        "volume": noise(arg_keys[0], (NH, ND, NX), 1.0, 6.0, ((0, 4), (1, 8)), jnp.float32),
        "measured": noise(arg_keys[1], (ANGLES, NH, NX), 2.0, 12.0, ((1, 4), (2, 8)), jnp.float32),
        "taps": jnp.clip(jnp.exp(math.log(0.1) - 2.3025851 * jax.random.uniform(arg_keys[2], (TAPS, ANGLES, ND), jnp.float32) ** levels(arg_keys[2], (TAPS, ANGLES, ND), ((2, 8),), -0.2, 0.2)), 0.01, 0.1),
        "band_offset": touch_ends(jax.random.randint(arg_keys[3], (ANGLES, BRICKS), -OFFMAX, OFFMAX + 1), jax.random.fold_in(arg_keys[3], 1), -OFFMAX, OFFMAX).astype(jnp.int32),
        "angle_index": touch_ends(jax.random.randint(arg_keys[4], (ANGLES,), 0, N_VIEWS), jax.random.fold_in(arg_keys[4], 1), 0, N_VIEWS - 1).astype(jnp.int32),
    }


relax_step = 0.5
tv_step = 0.08
tv_eps = 0.1

def cone_weights(taps, angle_index, first_slice, total_slices):
    slices = taps.shape[2]
    angle_value = 2.0 * math.pi / N_VIEWS * angle_index.astype(jnp.float32)
    depth_place = (first_slice + jnp.arange(slices, dtype=jnp.int32)).astype(jnp.float32) + 0.5
    rise = 0.5 + 0.45 * jnp.sin(angle_value)[:, None] * jnp.cos(math.pi / total_slices * depth_place)[None, :]
    return jnp.stack([taps * (1.0 - rise)[None], taps * rise[None]], axis=2)

def binary_shift(values, amount, toward):
    length = values.shape[-1]
    for bit_number in range((2 * OFFMAX).bit_length()):
        stride = 1 << bit_number
        zero_block = jnp.zeros(values.shape[:-1] + (stride,), values.dtype)
        if toward > 0:
            shifted = jnp.concatenate([zero_block, values[..., :length - stride]], axis=-1)
        else:
            shifted = jnp.concatenate([values[..., stride:], zero_block], axis=-1)
        chosen = amount // stride % 2 == 1
        values = jnp.where(chosen, shifted, values)
    return values

def project(block, factor, offsets):
    columns = block.shape[2]
    reach = 2 * OFFMAX
    term = jnp.einsum('kasy,hyx->kashx', factor, block, precision=lax.Precision.HIGHEST)
    padded = jnp.pad(term, ((0, 0), (0, 0), (0, 0), (0, 0), (OFFMAX + TAPS, OFFMAX)))
    window = columns + reach
    summed = padded[0, ..., TAPS:TAPS + window]
    for tap_number in range(1, TAPS):
        summed = summed + padded[tap_number, ..., TAPS - tap_number:TAPS - tap_number + window]
    amount = (offsets + OFFMAX).astype(jnp.int32)[:, None, None, None]
    shifted = binary_shift(summed, amount, 1)[..., reach:reach + columns]
    lower = jnp.pad(shifted[:, 0], ((0, 0), (0, 1), (0, 0)))
    upper = jnp.pad(shifted[:, 1], ((0, 0), (1, 0), (0, 0)))
    return lower + upper

def backproject(extended, factor, offsets):
    columns = extended.shape[2]
    layers = extended.shape[1] - 1
    padded = jnp.pad(extended, ((0, 0), (0, 0), (OFFMAX, OFFMAX + TAPS)))
    amount = (offsets + OFFMAX).astype(jnp.int32)[:, None, None]
    shifted = binary_shift(padded, amount, -1)
    moved = jnp.stack([shifted[..., tap_number:tap_number + columns] for tap_number in range(TAPS)], axis=0)
    stacked = jnp.stack([moved[:, :, :layers], moved[:, :, 1:]], axis=2)
    return jnp.einsum('kasy,kashx->hyx', factor, stacked, precision=lax.Precision.HIGHEST)

def forward(values, dimension, allowed):
    length = values.shape[dimension]
    following = jnp.concatenate([lax.slice_in_dim(values, 1, length, axis=dimension), lax.slice_in_dim(values, length - 1, length, axis=dimension)], axis=dimension)
    return jnp.where(allowed, following - values, 0.0)

def backward(normal, dimension):
    length = normal.shape[dimension]
    before = jnp.concatenate([jnp.zeros_like(lax.slice_in_dim(normal, 0, 1, axis=dimension)), lax.slice_in_dim(normal, 0, length - 1, axis=dimension)], axis=dimension)
    return normal - before

def allowed_mask(positions, total):
    return (positions >= 0) & (positions + 1 < total)

def tv_sweep(values, height_place, depth_place, width_place, height_total, depth_total, width_total):
    along_h = forward(values, 0, allowed_mask(height_place, height_total)[:, None, None])
    along_d = forward(values, 1, allowed_mask(depth_place, depth_total)[None, :, None])
    along_w = forward(values, 2, allowed_mask(width_place, width_total)[None, None, :])
    inverse = 1.0 / jnp.sqrt(tv_eps * tv_eps + along_h * along_h + along_d * along_d + along_w * along_w)
    diverge = backward(along_h * inverse, 0) + backward(along_d * inverse, 1) + backward(along_w * inverse, 2)
    return values + tv_step * diverge

def reference(volume, measured, taps, band_offset, angle_index):
    factor = cone_weights(taps, angle_index, 0, ND)
    bricks = jnp.arange(N_DEPTH, dtype=jnp.int32)

    def brick_image(image, brick):
        start = (brick * CD).astype(jnp.int32)
        block = lax.dynamic_slice_in_dim(volume, start, CD, 1)
        weights_part = lax.dynamic_slice_in_dim(factor, start, CD, 3)
        offsets = lax.dynamic_slice_in_dim(band_offset, brick, 1, 1)[:, 0]
        return (image + project(block, weights_part, offsets), None)
    image, _ = lax.scan(brick_image, jnp.zeros((ANGLES, NH + 1, NX), jnp.float32), bricks)
    residual = measured - image[:, :NH]
    extended = jnp.concatenate([residual, jnp.zeros((ANGLES, 1, NX), jnp.float32)], axis=1)

    def brick_update(carry, brick):
        start = (brick * CD).astype(jnp.int32)
        weights_part = lax.dynamic_slice_in_dim(factor, start, CD, 3)
        offsets = lax.dynamic_slice_in_dim(band_offset, brick, 1, 1)[:, 0]
        return (carry, backproject(extended, weights_part, offsets))
    _, blocks = lax.scan(brick_update, jnp.zeros((), jnp.float32), bricks)
    update = jnp.transpose(blocks, (1, 0, 2, 3)).reshape(NH, ND, NX)
    values = volume + relax_step * update
    height_place = jnp.arange(NH, dtype=jnp.int32)
    depth_place = jnp.arange(ND, dtype=jnp.int32)
    width_place = jnp.arange(NX, dtype=jnp.int32)
    for sweep_index in range(SWEEPS):
        values = tv_sweep(values, height_place, depth_place, width_place, NH, ND, NX)
    return values
```

```python
import math

import jax
import jax.numpy as jnp
from jax import lax
from jax.experimental import pallas as pl
from jax.experimental.pallas import tpu as pltpu
from jax.sharding import PartitionSpec as P

OFFMAX = 64
N_VIEWS = 720
SWEEPS = 2
LANES = 128
SUB = 8

relax_step = 0.5
tv_step = 0.08
tv_eps = 0.1

VMEM = pl.BlockSpec(memory_space=pltpu.VMEM)
SMEM = pl.BlockSpec(memory_space=pltpu.SMEM)


def up_to(value, unit):
    return -(-value // unit) * unit


class Sizes:
    def __init__(self, volume, measured, taps, depth_count, height_count):
        self.depth, self.height = depth_count, height_count
        self.layers, self.slices, self.columns = volume.shape
        self.taps, self.angles = taps.shape[:2]
        self.band = self.columns // depth_count
        self.total_slices = self.slices * depth_count
        self.left = OFFMAX + SWEEPS
        self.width = self.band + 2 * SWEEPS + 2 * OFFMAX + self.taps - 1
        self.vol_left = self.left + OFFMAX + self.taps - 1
        self.vol_width = self.width + 2 * OFFMAX + self.taps - 1
        self.field = self.band + 2 * SWEEPS
        self.width_p = up_to(self.width, LANES)
        self.vol_p = up_to(self.vol_width, LANES)
        self.field_p = up_to(self.field + self.taps - 1, LANES)
        self.pieces = []
        for away in range(-depth_count + 1, depth_count):
            first = max(0, away * self.band - self.left)
            last = min(self.band, self.width + away * self.band - self.left)
            if last > first:
                self.pieces.append((away, first, last))
        self.reach = max(abs(piece[0]) for piece in self.pieces)
        self.piece_p = max(
            [last - first for away, first, last in self.pieces if away != 0] + [1]
        )
        self.tap_lanes = self.taps * self.slices
        self.aligned = self.vol_width // LANES * LANES
        self.tap_at = self.vol_width - self.aligned
        self.piece_at = self.tap_at + self.tap_lanes
        self.message = up_to(
            self.vol_width + self.tap_lanes + self.layers * self.piece_p, LANES
        )
        self.extra = self.message - self.aligned
        self.rows = self.layers * self.slices


def lane_index(shape):
    return lax.broadcasted_iota(jnp.int32, shape, len(shape) - 1)


def roll_left(value, amount):
    width = value.shape[-1]
    amount = amount % width
    return value if amount == 0 else pltpu.roll(value, width - amount, value.ndim - 1)


def split(value):
    high = value.astype(jnp.bfloat16).astype(jnp.float32)
    return high, value - high


def pack_kernel(z, me_ref, volume_ref, extra_ref, out_ref):
    front = up_to(z.vol_left, LANES)
    back = up_to(z.vol_p + LANES, LANES)
    padded = jnp.concatenate(
        [
            jnp.zeros((z.rows, front), jnp.float32),
            volume_ref[...],
            jnp.zeros((z.rows, back), jnp.float32),
        ],
        axis=1,
    )
    me = me_ref[0]
    rolled = {}
    lane = lane_index((z.rows, LANES))
    for target in range(z.depth):
        start = front + target * z.band - z.vol_left
        shift = start % LANES
        if shift not in rolled:
            rolled[shift] = roll_left(padded, shift)
        begin = start - shift
        out_ref[target, :, : z.aligned] = rolled[shift][:, begin : begin + z.aligned]
        away = jnp.clip(target - me, -z.reach, z.reach) + z.reach
        extra = extra_ref[away]
        tail = rolled[shift][:, begin + z.aligned : begin + z.aligned + LANES]
        out_ref[target, :, z.aligned : z.aligned + LANES] = jnp.where(
            lane < z.tap_at, tail, extra[:, :LANES]
        )
        if z.extra > LANES:
            out_ref[target, :, z.aligned + LANES :] = extra[:, LANES:]


def tap_rows(z, message_ref, brick):
    tile = roll_left(
        message_ref[brick, : z.angles, z.aligned : z.aligned + LANES], z.tap_at
    )
    tile = jnp.where(lane_index(tile.shape) < z.tap_lanes, tile, 0.0)
    period = z.tap_lanes
    while period < LANES:
        tile = tile + pltpu.roll(tile, period, 1)
        period *= 2
    return tile


def spread_rows(z, low, high):
    width = low.shape[1]
    layer = lane_index((SUB, width)) % (z.layers * z.tap_lanes) // z.tap_lanes
    row = lax.broadcasted_iota(jnp.int32, (SUB, width), 0)
    same, above = row == layer, row == layer + 1
    blocks = []
    for angle in range(z.angles):
        first = jnp.broadcast_to(low[angle : angle + 1], (SUB, width))
        second = jnp.broadcast_to(high[angle : angle + 1], (SUB, width))
        blocks.append(jnp.where(same, first, jnp.where(above, second, 0.0)))
    return jnp.concatenate(blocks, axis=0)


def project_kernel(z, me_ref, offset_ref, message_ref, own_ref, sine_ref, cosine_ref, out_ref, sum_ref):
    me = me_ref[0]
    inner = z.layers * z.tap_lanes
    segment_lanes = up_to(3 * inner, LANES)
    sum_ref[...] = jnp.zeros_like(sum_ref)

    def brick_step(brick, carry):
        taps = tap_rows(z, message_ref, brick)
        taps = jnp.concatenate([taps] * (segment_lanes // LANES), axis=1)
        rise = 0.5 + 0.45 * sine_ref[...] * cosine_ref[brick]
        middle = lane_index(taps.shape) // inner == 1
        parts = []
        for weight in (taps * (1.0 - rise), taps * rise):
            high, low = split(weight)
            parts.append(jnp.where(middle, low, high))
        left = spread_rows(z, parts[0], parts[1])[:, : 3 * inner].astype(jnp.bfloat16)
        highs, lows = [], []
        for layer in range(z.layers):
            block = message_ref[brick, layer * z.slices : (layer + 1) * z.slices, : z.vol_p]
            high, low = split(block)
            for tap in range(z.taps):
                highs.append(pltpu.roll(high, tap, 1) if tap else high)
                lows.append(pltpu.roll(low, tap, 1) if tap else low)
        high = jnp.concatenate(highs, axis=0).astype(jnp.bfloat16)
        low = jnp.concatenate(lows, axis=0).astype(jnp.bfloat16)
        product = jnp.dot(
            left,
            jnp.concatenate([high, high, low], axis=0),
            preferred_element_type=jnp.float32,
        )
        for angle in range(z.angles):
            amount = z.vol_p - (OFFMAX + z.taps - 1) + offset_ref[angle, brick]
            moved = pltpu.roll(product[angle * SUB : (angle + 1) * SUB], amount, 1)
            for tile in range(z.width_p // LANES):
                rows = pl.ds((tile * z.angles + angle) * SUB, SUB)
                sum_ref[rows, :] = sum_ref[rows, :] + moved[:, tile * LANES : (tile + 1) * LANES]
        return carry

    lax.fori_loop(0, z.depth, brick_step, 0)
    lane = lane_index((z.angles, z.width_p))
    column = me * z.band - z.left + lane
    inside = (column >= 0) & (column < z.columns)
    for row in range(z.layers + 1):
        total = -jnp.concatenate(
            [
                sum_ref[pl.ds(tile * z.angles * SUB + row, z.angles, SUB), :]
                for tile in range(z.width_p // LANES)
            ],
            axis=1,
        )
        if row < z.layers:
            window = own_ref[row]
            for away, first, last in z.pieces:
                if away == 0:
                    continue
                source = jnp.clip(me - away, 0, z.depth - 1)
                tail = message_ref[source, : z.angles, z.aligned :]
                if z.extra < z.width_p:
                    tail = jnp.concatenate(
                        [tail, jnp.zeros((z.angles, z.width_p - z.extra), jnp.float32)], axis=1
                    )
                else:
                    tail = tail[:, : z.width_p]
                begin = first - away * z.band + z.left
                tail = roll_left(tail, z.piece_at + row * z.piece_p - begin)
                here = (lane >= begin) & (lane < begin + last - first)
                window = jnp.where(here, tail, window)
            total = total + window
        out_ref[row] = jnp.where(inside, total, 0.0)


def adjoint_kernel(z, message_ref, sine_ref, cosine_ref, out_ref):
    inner = z.layers * z.tap_lanes

    def brick_step(brick, carry):
        taps = tap_rows(z, message_ref, brick)
        rise = 0.5 + 0.45 * sine_ref[:, :LANES] * cosine_ref[brick, :, :LANES]
        spread = spread_rows(z, taps * (1.0 - rise), taps * rise)
        high, low = split(spread.T[:inner])
        out_ref[brick] = jnp.concatenate([high, low, high], axis=1).astype(jnp.bfloat16)
        return carry

    lax.fori_loop(0, z.depth, brick_step, 0)


def backproject_kernel(z, place_ref, offset_ref, own_ref, below_ref, above_ref, message_ref, weight_ref, out_ref, row_ref):
    row_ref[...] = jnp.zeros_like(row_ref)
    last = place_ref[1] == z.height - 1
    for row in range(z.layers + 1):
        value = own_ref[row]
        if row == 0:
            value = value + below_ref[...]
        if row == z.layers:
            value = jnp.where(last, 0.0, value + above_ref[...])
        for tile in range(z.width_p // LANES):
            row_ref[pl.ds(tile * z.angles * SUB + row, z.angles, SUB), :] = value[
                :, tile * LANES : (tile + 1) * LANES
            ]
    lead = z.vol_left - SWEEPS

    def brick_step(brick, carry):
        blocks = []
        for angle in range(z.angles):
            amount = (z.width_p - OFFMAX - offset_ref[angle, brick]) % z.width_p
            block = jnp.concatenate(
                [
                    row_ref[pl.ds((tile * z.angles + angle) * SUB, SUB), :]
                    for tile in range(z.width_p // LANES)
                ],
                axis=1,
            )
            block = pltpu.roll(block, amount, 1)
            blocks.append(block[:, : z.field_p])
        high, low = split(jnp.concatenate(blocks, axis=0))
        high = high.astype(jnp.bfloat16)
        low = low.astype(jnp.bfloat16)
        product = jnp.dot(
            weight_ref[brick],
            jnp.concatenate([high, high, low], axis=0),
            preferred_element_type=jnp.float32,
        )
        for layer in range(z.layers):
            update = None
            for tap in range(z.taps):
                begin = (layer * z.taps + tap) * z.slices
                term = roll_left(product[begin : begin + z.slices], tap)
                update = term if update is None else update + term
            start = lead // LANES * LANES
            voxels = message_ref[
                brick, layer * z.slices : (layer + 1) * z.slices, start : start + z.field_p + LANES
            ]
            voxels = roll_left(voxels, lead - start)[:, : z.field_p]
            out_ref[layer, brick] = voxels + relax_step * update
        return carry

    lax.fori_loop(0, z.depth, brick_step, 0)


def denoise_kernel(z, place_ref, below_ref, own_ref, above_ref, out_ref):
    shape = (z.total_slices, z.field_p)
    column = place_ref[0] * z.band - SWEEPS + lane_index(shape)
    slice_at = lax.broadcasted_iota(jnp.int32, shape, 0)
    allow_x = (column >= 0) & (column + 1 < z.columns)
    allow_y = slice_at + 1 < z.total_slices
    not_first = slice_at > 0
    first_layer = place_ref[1] * z.layers
    values = {}
    for layer in range(-SWEEPS, z.layers + SWEEPS):
        if layer < 0:
            values[layer] = below_ref[z.layers + layer]
        elif layer < z.layers:
            values[layer] = own_ref[layer]
        else:
            values[layer] = above_ref[layer - z.layers]
    for sweep in range(SWEEPS):
        margin = SWEEPS - 1 - sweep
        later = {}
        before = None
        for layer in range(-margin - 1, z.layers + margin):
            here = values[layer]
            place = first_layer + layer
            allow_z = (place >= 0) & (place + 1 < z.height * z.layers)
            along_z = jnp.where(allow_z, values[layer + 1] - here, 0.0)
            along_y = jnp.where(allow_y, pltpu.roll(here, z.total_slices - 1, 0) - here, 0.0)
            along_x = jnp.where(allow_x, roll_left(here, 1) - here, 0.0)
            inverse = lax.rsqrt(
                tv_eps * tv_eps + along_z * along_z + along_y * along_y + along_x * along_x
            )
            normal_z = along_z * inverse
            if layer >= -margin:
                normal_y = along_y * inverse
                normal_x = along_x * inverse
                diverge = (
                    normal_z
                    - before
                    + normal_y
                    - jnp.where(not_first, pltpu.roll(normal_y, 1, 0), 0.0)
                    + normal_x
                    - pltpu.roll(normal_x, 1, 1)
                )
                later[layer] = here + tv_step * diverge
            before = normal_z
        values = later
    for layer in range(z.layers):
        result = roll_left(values[layer], SWEEPS)
        for brick in range(z.depth):
            out_ref[brick, layer] = result[brick * z.slices : (brick + 1) * z.slices, : z.band]


def shifted(value, axis, by):
    count = lax.axis_size(axis)
    pairs = [(i, i + by) for i in range(count) if 0 <= i + by < count]
    return lax.ppermute(value, axis, pairs)


def call(kernel, z, shape, specs, scratch=(), dtype=jnp.float32, cycles=2000):
    return pl.pallas_call(
        lambda *refs: kernel(z, *refs),
        out_shape=jax.ShapeDtypeStruct(shape, dtype),
        in_specs=specs,
        out_specs=VMEM,
        scratch_shapes=list(scratch),
        name=kernel.__name__,
    )


def per_device(volume, measured, taps, band_offset, angle_index):
    z = Sizes(volume, measured, taps, lax.axis_size("depth"), lax.axis_size("height"))
    depth_of = lax.axis_index("depth")
    height_of = lax.axis_index("height")
    place = jnp.stack([depth_of, height_of]).astype(jnp.int32)

    tap_part = jnp.transpose(taps, (1, 0, 2)).reshape(z.angles, z.tap_lanes)
    extras = []
    table = {away: (first, last) for away, first, last in z.pieces}
    for away in range(-z.reach, z.reach + 1):
        parts = [jnp.zeros((z.angles, z.tap_at), jnp.float32), tap_part]
        for row in range(z.layers):
            first, last = table[away] if away != 0 else (0, 0)
            piece = measured[:, row, first:last]
            parts.append(jnp.pad(piece, ((0, 0), (0, z.piece_p - (last - first)))))
        joined = jnp.concatenate(parts, axis=1)
        extras.append(jnp.pad(joined, ((0, z.rows - z.angles), (0, z.extra - joined.shape[1]))))
    extra = jnp.stack(extras)
    own = jnp.pad(
        jnp.transpose(measured, (1, 0, 2)),
        ((0, 0), (0, 0), (z.left, z.width_p - z.left - z.band)),
    )
    segment_lanes = up_to(3 * z.layers * z.tap_lanes, LANES)
    angle_value = 2.0 * math.pi / N_VIEWS * angle_index.astype(jnp.float32)
    sine = jnp.broadcast_to(jnp.sin(angle_value)[:, None], (z.angles, segment_lanes))
    slice_at = (
        jnp.arange(z.depth, dtype=jnp.int32)[:, None] * z.slices
        + jnp.arange(segment_lanes, dtype=jnp.int32)[None, :] % z.slices
    )
    cosine = jnp.cos(math.pi / z.total_slices * (slice_at.astype(jnp.float32) + 0.5))[:, None, :]

    message = call(pack_kernel, z, (z.depth, z.rows, z.message), [SMEM, VMEM, VMEM])(
        place, volume.reshape(z.rows, z.columns), extra
    )
    message = lax.all_to_all(message, "depth", 0, 0)
    partial = call(
        project_kernel,
        z,
        (z.layers + 1, z.angles, z.width_p),
        [SMEM, SMEM, VMEM, VMEM, VMEM, VMEM],
        [pltpu.VMEM((z.width_p // LANES * z.angles * SUB, LANES), jnp.float32)],
    )(place, band_offset, message, own, sine, cosine)
    below = shifted(partial[z.layers], "height", 1)
    above = shifted(partial[0], "height", -1)
    weight = call(
        adjoint_kernel,
        z,
        (z.depth, z.layers * z.tap_lanes, 3 * z.angles * SUB),
        [VMEM, VMEM, VMEM],
        dtype=jnp.bfloat16,
    )(message, sine, cosine)
    field = call(
        backproject_kernel,
        z,
        (z.layers, z.depth, z.slices, z.field_p),
        [SMEM, SMEM, VMEM, VMEM, VMEM, VMEM, VMEM],
        [pltpu.VMEM((z.width_p // LANES * z.angles * SUB, LANES), jnp.float32)],
    )(place, band_offset, partial, below, above, message, weight)
    field = field.reshape(z.layers, z.total_slices, z.field_p)
    field_below = shifted(field, "height", 1)
    field_above = shifted(field, "height", -1)
    bands = call(
        denoise_kernel,
        z,
        (z.depth, z.layers, z.slices, z.band),
        [SMEM, VMEM, VMEM, VMEM],
    )(place, field_below, field, field_above)
    bands = lax.all_to_all(bands, "depth", 0, 0)
    return jnp.transpose(bands, (1, 2, 0, 3)).reshape(volume.shape)


def solution(mesh):
    in_specs = (
        P("height", "depth", None),
        P(None, "height", "depth"),
        P(None, None, "depth"),
        P(),
        P(),
    )
    out_specs = P("height", "depth", None)
    return jax.shard_map(
        per_device, mesh=mesh, in_specs=in_specs, out_specs=out_specs, check_vma=False
    )
```

```python
import math

import jax
import jax.numpy as jnp
from jax import lax
from jax.experimental import pallas as pl
from jax.experimental.pallas import tpu as pltpu
from jax.sharding import PartitionSpec as P


OFFMAX = 64
N_VIEWS = 720
SWEEPS = 2
LANES = 128
SUB = 8

relax_step = 0.5
tv_step = 0.08
tv_eps = 0.1

VMEM = pl.BlockSpec(memory_space=pltpu.VMEM)
SMEM = pl.BlockSpec(memory_space=pltpu.SMEM)


def up_to(value, unit):
    return -(-value // unit) * unit


class Sizes:
    def __init__(self, volume, taps, depth_count, height_count):
        self.depth, self.height = depth_count, height_count
        self.layers, self.slices, self.columns = volume.shape
        self.taps, self.angles = taps.shape[:2]
        self.band = self.columns // depth_count
        self.total_slices = self.slices * depth_count
        self.left = OFFMAX + SWEEPS
        self.width = self.band + 2 * SWEEPS + 2 * OFFMAX + self.taps - 1
        self.vol_left = self.left + OFFMAX + self.taps - 1
        self.vol_width = self.width + 2 * OFFMAX + self.taps - 1
        self.field = self.band + 2 * SWEEPS
        self.width_p = up_to(self.width, LANES)
        self.vol_p = up_to(self.vol_width, LANES)
        self.field_p = up_to(self.field + self.taps - 1, LANES)
        self.pieces = []
        for away in range(-depth_count + 1, depth_count):
            first = max(0, away * self.band - self.left)
            last = min(self.band, self.width + away * self.band - self.left)
            if last > first:
                self.pieces.append((away, first, last))
        self.piece_p = max(
            [last - first for away, first, last in self.pieces if away != 0] + [1]
        )
        self.tap_lanes = self.taps * self.slices
        self.aligned = self.vol_width // LANES * LANES
        self.tap_at = self.vol_width - self.aligned
        self.message = up_to(self.vol_width + self.tap_lanes, LANES)
        self.piece_p = up_to(self.piece_p, LANES)
        self.rows = self.layers * self.slices


def lane_index(shape):
    return lax.broadcasted_iota(jnp.int32, shape, len(shape) - 1)


def roll_left(value, amount):
    width = value.shape[-1]
    amount = amount % width
    return value if amount == 0 else pltpu.roll(value, width - amount, value.ndim - 1)


def shift_tiles(tiles, amount, count):
    turned = pltpu.roll(jnp.concatenate(tiles, axis=0), (LANES - amount) % LANES, 1)
    keep = lane_index((SUB, LANES)) < LANES - amount
    return [
        jnp.where(keep, turned[i * SUB : (i + 1) * SUB], turned[(i + 1) * SUB : (i + 2) * SUB])
        for i in range(count)
    ]


def for_bricks(z, step):
    unroll = next(u for u in (8, 4, 2, 1) if z.depth % u == 0)
    if unroll == z.depth:
        for brick in range(z.depth):
            step(brick)
        return

    def several(start, carry):
        for inner in range(unroll):
            step(start * unroll + inner)
        return carry

    lax.fori_loop(0, z.depth // unroll, several, 0)


def split(value):
    high = value.astype(jnp.bfloat16).astype(jnp.float32)
    return high, value - high


def pack_kernel(z, volume_ref, taps_ref, out_ref):
    front = up_to(z.vol_left, LANES)
    back = up_to(z.message + LANES, LANES)
    padded = jnp.concatenate(
        [
            jnp.zeros((z.rows, front), jnp.float32),
            volume_ref[...],
            jnp.zeros((z.rows, back), jnp.float32),
        ],
        axis=1,
    )
    block = jnp.concatenate(
        [taps_ref[...], jnp.zeros((z.tap_lanes, LANES - z.angles), jnp.float32)], axis=1
    )
    block = jnp.concatenate(
        [block, jnp.zeros((LANES - z.tap_lanes, LANES), jnp.float32)], axis=0
    )
    block = block.T[: z.rows]
    block = jnp.concatenate(
        [block, jnp.zeros((z.rows, z.message - z.aligned - LANES + LANES), jnp.float32)], axis=1
    )
    tail_width = z.message - z.aligned
    block = roll_left(block, -z.tap_at)[:, :tail_width]
    keep = lane_index((z.rows, tail_width)) < z.tap_at
    rolled = {}
    for target in range(z.depth):
        start = front + target * z.band - z.vol_left
        shift = start % LANES
        if shift not in rolled:
            rolled[shift] = roll_left(padded, shift)
        begin = start - shift
        out_ref[target, :, : z.aligned] = rolled[shift][:, begin : begin + z.aligned]
        tail = rolled[shift][:, begin + z.aligned : begin + z.message]
        out_ref[target, :, z.aligned :] = jnp.where(keep, tail, block)


def tap_rows(z, message_ref, brick):
    tile = roll_left(
        message_ref[brick, : z.angles, z.aligned : z.aligned + LANES], z.tap_at
    )
    tile = jnp.where(lane_index(tile.shape) < z.tap_lanes, tile, 0.0)
    period = z.tap_lanes
    while period < LANES:
        tile = tile + pltpu.roll(tile, period, 1)
        period *= 2
    return tile


def spread_rows(z, low, high):
    width = low.shape[1]
    layer = lane_index((SUB, width)) % (z.layers * z.tap_lanes) // z.tap_lanes
    row = lax.broadcasted_iota(jnp.int32, (SUB, width), 0)
    same, above = row == layer, row == layer + 1
    blocks = []
    for angle in range(z.angles):
        first = jnp.broadcast_to(low[angle : angle + 1], (SUB, width))
        second = jnp.broadcast_to(high[angle : angle + 1], (SUB, width))
        blocks.append(jnp.where(same, first, jnp.where(above, second, 0.0)))
    return jnp.concatenate(blocks, axis=0)


def project_kernel(z, me_ref, offset_ref, message_ref, own_ref, sine_ref, cosine_ref, *refs):
    *piece_refs, out_ref, sum_ref = refs
    me = me_ref[0]
    inner = z.layers * z.tap_lanes
    segment_lanes = up_to(3 * inner, LANES)
    sum_ref[...] = jnp.zeros_like(sum_ref)
    count = z.width_p // LANES

    def brick_step(brick):
        taps = tap_rows(z, message_ref, brick)
        taps = jnp.concatenate([taps] * (segment_lanes // LANES), axis=1)
        rise = 0.5 + 0.45 * sine_ref[...] * cosine_ref[brick]
        middle = lane_index(taps.shape) // inner == 1
        parts = []
        for weight in (taps * (1.0 - rise), taps * rise):
            high, low = split(weight)
            parts.append(jnp.where(middle, low, high))
        left = spread_rows(z, parts[0], parts[1])[:, : 3 * inner].astype(jnp.bfloat16)
        highs, lows = [], []
        for layer in range(z.layers):
            block = message_ref[brick, layer * z.slices : (layer + 1) * z.slices, : z.vol_p]
            high, low = split(block)
            for tap in range(z.taps):
                highs.append(roll_left(high, z.taps - 1 - tap))
                lows.append(roll_left(low, z.taps - 1 - tap))
        high = jnp.concatenate(highs, axis=0).astype(jnp.bfloat16)
        low = jnp.concatenate(lows, axis=0).astype(jnp.bfloat16)
        product = jnp.dot(
            left,
            jnp.concatenate([high, high, low], axis=0),
            preferred_element_type=jnp.float32,
        )
        for angle in range(z.angles):
            tiles = [
                product[angle * SUB : (angle + 1) * SUB, tile * LANES : (tile + 1) * LANES]
                for tile in range(count + 1)
            ]
            moved = shift_tiles(tiles, OFFMAX - offset_ref[angle, brick], count)
            for tile in range(count):
                rows = pl.ds((tile * z.angles + angle) * SUB, SUB)
                sum_ref[rows, :] = sum_ref[rows, :] + moved[tile]

    for_bricks(z, brick_step)
    lane = lane_index((z.angles, z.width_p))
    column = me * z.band - z.left + lane
    inside = (column >= 0) & (column < z.columns)
    for row in range(z.layers + 1):
        total = -jnp.concatenate(
            [
                sum_ref[pl.ds(tile * z.angles * SUB + row, z.angles, SUB), :]
                for tile in range(z.width_p // LANES)
            ],
            axis=1,
        )
        if row < z.layers:
            window = own_ref[row]
            order = 0
            for away, first, last in z.pieces:
                if away == 0:
                    continue
                tail = piece_refs[order][row * z.angles : (row + 1) * z.angles]
                order += 1
                tail = jnp.concatenate(
                    [tail, jnp.zeros((z.angles, z.width_p - z.piece_p), jnp.float32)], axis=1
                )
                begin = first - away * z.band + z.left
                tail = roll_left(tail, -begin)
                here = (lane >= begin) & (lane < begin + last - first)
                window = jnp.where(here, tail, window)
            total = total + window
        out_ref[row] = jnp.where(inside, total, 0.0)


def adjoint_kernel(z, message_ref, sine_ref, cosine_ref, out_ref):
    inner = z.layers * z.tap_lanes

    def brick_step(brick):
        taps = tap_rows(z, message_ref, brick)
        rise = 0.5 + 0.45 * sine_ref[:, :LANES] * cosine_ref[brick, :, :LANES]
        spread = spread_rows(z, taps * (1.0 - rise), taps * rise)
        high, low = split(spread.T[:inner])
        out_ref[brick] = jnp.concatenate([high, low, high], axis=1).astype(jnp.bfloat16)

    for_bricks(z, brick_step)


def backproject_kernel(z, place_ref, offset_ref, own_ref, near_ref, far_ref, message_ref, weight_ref, out_ref, row_ref):
    row_ref[...] = jnp.zeros_like(row_ref)
    last = place_ref[1] == z.height - 1
    even = place_ref[1] % 2 == 0
    below = jnp.where(even, far_ref[...], near_ref[...])
    above = jnp.where(even, near_ref[...], far_ref[...])
    for row in range(z.layers + 1):
        value = own_ref[row]
        if row == 0:
            value = value + below
        if row == z.layers:
            value = jnp.where(last, 0.0, value + above)
        for tile in range(z.width_p // LANES):
            row_ref[pl.ds(tile * z.angles * SUB + row, z.angles, SUB), :] = value[
                :, tile * LANES : (tile + 1) * LANES
            ]
    lead = z.vol_left - SWEEPS

    count = z.field_p // LANES

    def brick_step(brick):
        blocks = []
        for angle in range(z.angles):
            tiles = [
                row_ref[pl.ds((tile * z.angles + angle) * SUB, SUB), :]
                for tile in range(count + 1)
            ]
            moved = shift_tiles(tiles, OFFMAX + offset_ref[angle, brick], count)
            blocks.append(jnp.concatenate(moved, axis=1))
        high, low = split(jnp.concatenate(blocks, axis=0))
        high = high.astype(jnp.bfloat16)
        low = low.astype(jnp.bfloat16)
        product = jnp.dot(
            weight_ref[brick],
            jnp.concatenate([high, high, low], axis=0),
            preferred_element_type=jnp.float32,
        )
        for layer in range(z.layers):
            update = None
            for tap in range(z.taps):
                begin = (layer * z.taps + tap) * z.slices
                term = roll_left(product[begin : begin + z.slices], tap)
                update = term if update is None else update + term
            start = lead // LANES * LANES
            voxels = message_ref[
                brick, layer * z.slices : (layer + 1) * z.slices, start : start + z.field_p + LANES
            ]
            voxels = roll_left(voxels, lead - start)[:, : z.field_p]
            out_ref[layer, brick] = voxels + relax_step * update

    for_bricks(z, brick_step)


def denoise_kernel(z, place_ref, near_ref, own_ref, far_ref, out_ref):
    shape = (z.total_slices, z.field_p)
    column = place_ref[0] * z.band - SWEEPS + lane_index(shape)
    slice_at = lax.broadcasted_iota(jnp.int32, shape, 0)
    allow_x = (column >= 0) & (column + 1 < z.columns)
    allow_y = slice_at + 1 < z.total_slices
    not_first = slice_at > 0
    first_layer = place_ref[1] * z.layers
    even = place_ref[1] % 2 == 0
    values = {}
    for layer in range(-SWEEPS, z.layers + SWEEPS):
        if layer < 0:
            values[layer] = jnp.where(
                even, far_ref[z.layers + layer], near_ref[z.layers + layer]
            )
        elif layer < z.layers:
            values[layer] = own_ref[layer]
        else:
            values[layer] = jnp.where(
                even, near_ref[layer - z.layers], far_ref[layer - z.layers]
            )
    for sweep in range(SWEEPS):
        margin = SWEEPS - 1 - sweep
        later = {}
        before = None
        for layer in range(-margin - 1, z.layers + margin):
            here = values[layer]
            place = first_layer + layer
            allow_z = (place >= 0) & (place + 1 < z.height * z.layers)
            along_z = jnp.where(allow_z, values[layer + 1] - here, 0.0)
            along_y = jnp.where(allow_y, pltpu.roll(here, z.total_slices - 1, 0) - here, 0.0)
            along_x = jnp.where(allow_x, roll_left(here, 1) - here, 0.0)
            inverse = lax.rsqrt(
                tv_eps * tv_eps + along_z * along_z + along_y * along_y + along_x * along_x
            )
            normal_z = along_z * inverse
            if layer >= -margin:
                normal_y = along_y * inverse
                normal_x = along_x * inverse
                diverge = (
                    normal_z
                    - before
                    + normal_y
                    - jnp.where(not_first, pltpu.roll(normal_y, 1, 0), 0.0)
                    + normal_x
                    - pltpu.roll(normal_x, 1, 1)
                )
                later[layer] = here + tv_step * diverge
            before = normal_z
        values = later
    for layer in range(z.layers):
        result = roll_left(values[layer], SWEEPS)
        for brick in range(z.depth):
            out_ref[brick, layer] = result[brick * z.slices : (brick + 1) * z.slices, : z.band]


def shifted(value, axis, by):
    count = lax.axis_size(axis)
    pairs = [(i, i + by) for i in range(count) if 0 <= i + by < count]
    return lax.ppermute(value, axis, pairs)


def swapped(value, axis, first):
    count = lax.axis_size(axis)
    pairs = []
    for low in range(first, count - 1, 2):
        pairs += [(low, low + 1), (low + 1, low)]
    return lax.ppermute(value, axis, pairs)


def call(kernel, z, shape, specs, scratch=(), dtype=jnp.float32, limit=16 << 20):
    return pl.pallas_call(
        lambda *refs: kernel(z, *refs),
        out_shape=jax.ShapeDtypeStruct(shape, dtype),
        in_specs=specs,
        out_specs=VMEM,
        scratch_shapes=list(scratch),
        compiler_params=pltpu.CompilerParams(vmem_limit_bytes=limit),
    )


def per_device(volume, measured, taps, band_offset, angle_index):
    z = Sizes(volume, taps, lax.axis_size("depth"), lax.axis_size("height"))
    depth_of = lax.axis_index("depth")
    height_of = lax.axis_index("height")
    place = jnp.stack([depth_of, height_of]).astype(jnp.int32)

    pieces = []
    for away, first, last in z.pieces:
        if away == 0:
            continue
        piece = jnp.transpose(measured[:, :, first:last], (1, 0, 2))
        piece = jnp.pad(piece, ((0, 0), (0, 0), (0, z.piece_p - (last - first))))
        piece = piece.reshape(z.layers * z.angles, z.piece_p)
        pieces.append(shifted(piece, "depth", away))
    own = jnp.pad(
        jnp.transpose(measured, (1, 0, 2)),
        ((0, 0), (0, 0), (z.left, z.width_p - z.left - z.band)),
    )
    segment_lanes = up_to(3 * z.layers * z.tap_lanes, LANES)
    angle_value = 2.0 * math.pi / N_VIEWS * angle_index.astype(jnp.float32)
    sine = jnp.broadcast_to(jnp.sin(angle_value)[:, None], (z.angles, segment_lanes))
    slice_at = (
        jnp.arange(z.depth, dtype=jnp.int32)[:, None] * z.slices
        + jnp.arange(segment_lanes, dtype=jnp.int32)[None, :] % z.slices
    )
    cosine = jnp.cos(math.pi / z.total_slices * (slice_at.astype(jnp.float32) + 0.5))[:, None, :]

    message = call(
        pack_kernel, z, (z.depth, z.rows, z.message), [VMEM, VMEM], limit=None
    )(
        volume.reshape(z.rows, z.columns),
        jnp.transpose(taps, (0, 2, 1)).reshape(z.tap_lanes, z.angles),
    )
    message = lax.all_to_all(message, "depth", 0, 0)
    partial = call(
        project_kernel,
        z,
        (z.layers + 1, z.angles, z.width_p),
        [SMEM, SMEM, VMEM, VMEM, VMEM, VMEM] + [VMEM] * len(pieces),
        [pltpu.VMEM((z.width_p // LANES * z.angles * SUB, LANES), jnp.float32)],
    )(place, band_offset, message, own, sine, cosine, *pieces)
    even = height_of % 2 == 0
    upward, downward = partial[z.layers], partial[0]
    far = swapped(jnp.where(even, downward, upward), "height", 1)
    near = swapped(jnp.where(even, upward, downward), "height", 0)
    weight = call(
        adjoint_kernel,
        z,
        (z.depth, z.layers * z.tap_lanes, 3 * z.angles * SUB),
        [VMEM, VMEM, VMEM],
        dtype=jnp.bfloat16,
    )(message, sine, cosine)
    field = call(
        backproject_kernel,
        z,
        (z.layers, z.depth, z.slices, z.field_p),
        [SMEM, SMEM, VMEM, VMEM, VMEM, VMEM, VMEM],
        [pltpu.VMEM((z.width_p // LANES * z.angles * SUB, LANES), jnp.float32)],
    )(place, band_offset, partial, near, far, message, weight)
    field = field.reshape(z.layers, z.total_slices, z.field_p)
    field_far = swapped(field, "height", 1)
    field_near = swapped(field, "height", 0)
    bands = call(
        denoise_kernel,
        z,
        (z.depth, z.layers, z.slices, z.band),
        [SMEM, VMEM, VMEM, VMEM],
    )(place, field_near, field, field_far)
    bands = lax.all_to_all(bands, "depth", 0, 0)
    return jnp.transpose(bands, (1, 2, 0, 3)).reshape(volume.shape)


def solution(mesh):
    in_specs = (
        P("height", "depth", None),
        P(None, "height", "depth"),
        P(None, None, "depth"),
        P(),
        P(),
    )
    out_specs = P("height", "depth", None)

    return jax.shard_map(
        per_device, mesh=mesh, in_specs=in_specs, out_specs=out_specs, check_vma=False
    )
```

```python
import math

import jax
import jax.numpy as jnp
from jax import lax
from jax.experimental import pallas as pl
from jax.experimental.pallas import tpu as pltpu
from jax.sharding import PartitionSpec as P


OFFMAX = 64
N_VIEWS = 720
SWEEPS = 2
LANES = 128
SUB = 8

relax_step = 0.5
tv_step = 0.08
tv_eps = 0.1

VMEM = pl.BlockSpec(memory_space=pltpu.VMEM)
SMEM = pl.BlockSpec(memory_space=pltpu.SMEM)


def up_to(value, unit):
    return -(-value // unit) * unit


class Sizes:
    def __init__(self, volume, taps, depth_count, height_count):
        self.depth, self.height = depth_count, height_count
        self.layers, self.slices, self.columns = volume.shape
        self.taps, self.angles = taps.shape[:2]
        self.band = self.columns // depth_count
        self.total_slices = self.slices * depth_count
        self.left = OFFMAX + SWEEPS
        self.width = self.band + 2 * SWEEPS + 2 * OFFMAX + self.taps - 1
        self.vol_left = self.left + OFFMAX + self.taps - 1
        self.vol_width = self.width + 2 * OFFMAX + self.taps - 1
        self.field = self.band + 2 * SWEEPS
        self.width_p = up_to(self.width, LANES)
        self.lead = self.vol_left - SWEEPS
        self.lag = self.lead % LANES
        self.field_p = up_to(self.field + self.lag, LANES)
        self.half = -(-self.width_p // LANES // 2)
        self.margin = SWEEPS
        self.near_layers = self.layers + 2 * self.margin
        if self.layers != self.margin or self.lag != self.taps - 1:
            raise ValueError("unsupported sizes")
        self.pieces = []
        for away in range(-depth_count + 1, depth_count):
            first = max(0, away * self.band - self.left)
            last = min(self.band, self.width + away * self.band - self.left)
            if last > first:
                self.pieces.append((away, first, last))
        self.piece_p = max(
            [last - first for away, first, last in self.pieces if away != 0] + [1]
        )
        self.tap_lanes = self.taps * self.slices
        self.aligned = self.vol_width // LANES * LANES
        self.tap_at = self.vol_width - self.aligned
        self.message = up_to(self.vol_width + self.tap_lanes, LANES)
        self.message = max(self.message, (2 * self.half + 1) * LANES)
        self.piece_p = up_to(self.piece_p, LANES)
        self.rows = self.layers * self.slices


def lane_index(shape):
    return lax.broadcasted_iota(jnp.int32, shape, len(shape) - 1)


def roll_left(value, amount):
    width = value.shape[-1]
    amount = amount % width
    return value if amount == 0 else pltpu.roll(value, width - amount, value.ndim - 1)


def shift_tiles(tiles, amount, count):
    turned = pltpu.roll(jnp.concatenate(tiles, axis=0), (LANES - amount) & (LANES - 1), 1)
    keep = lane_index((SUB, LANES)) < LANES - amount
    return [
        jnp.where(keep, turned[i * SUB : (i + 1) * SUB], turned[(i + 1) * SUB : (i + 2) * SUB])
        for i in range(count)
    ]


def for_bricks(z, step):
    unroll = next(u for u in (8, 4, 2, 1) if z.depth % u == 0)
    if unroll == z.depth:
        for brick in range(z.depth):
            step(brick)
        return

    def several(start, carry):
        for inner in range(unroll):
            step(start * unroll + inner)
        return carry

    lax.fori_loop(0, z.depth // unroll, several, 0)


def split(value):
    high = value.astype(jnp.bfloat16).astype(jnp.float32)
    return high, value - high


def pack_kernel(z, volume_ref, taps_ref, out_ref):
    front = up_to(z.vol_left, LANES)
    back = up_to(z.message + LANES, LANES)
    padded = jnp.concatenate(
        [
            jnp.zeros((z.rows, front), jnp.float32),
            volume_ref[...],
            jnp.zeros((z.rows, back), jnp.float32),
        ],
        axis=1,
    )
    block = jnp.concatenate(
        [taps_ref[...], jnp.zeros((z.tap_lanes, LANES - z.angles), jnp.float32)], axis=1
    )
    block = jnp.concatenate(
        [block, jnp.zeros((LANES - z.tap_lanes, LANES), jnp.float32)], axis=0
    )
    block = block.T[: z.rows]
    block = jnp.concatenate(
        [block, jnp.zeros((z.rows, z.message - z.aligned - LANES + LANES), jnp.float32)], axis=1
    )
    tail_width = z.message - z.aligned
    block = roll_left(block, -z.tap_at)[:, :tail_width]
    keep = lane_index((z.rows, tail_width)) < z.tap_at
    rolled = {}
    for target in range(z.depth):
        start = front + target * z.band - z.vol_left
        shift = start % LANES
        if shift not in rolled:
            rolled[shift] = roll_left(padded, shift)
        begin = start - shift
        out_ref[target, :, : z.aligned] = rolled[shift][:, begin : begin + z.aligned]
        tail = rolled[shift][:, begin + z.aligned : begin + z.message]
        out_ref[target, :, z.aligned :] = jnp.where(keep, tail, block)


def tap_rows(z, message_ref, brick):
    tile = roll_left(
        message_ref[brick, : z.angles, z.aligned : z.aligned + LANES], z.tap_at
    )
    tile = jnp.where(lane_index(tile.shape) < z.tap_lanes, tile, 0.0)
    period = z.tap_lanes
    while period < LANES:
        tile = tile + pltpu.roll(tile, period, 1)
        period *= 2
    return tile


def row_masks(lane_layer, lane_segment):
    row = lax.broadcasted_iota(jnp.int32, lane_layer.shape, 0)
    inside = lane_segment == row // 4
    return inside & (row % 4 == lane_layer), inside & (row % 4 == lane_layer + 1)


def project_kernel(z, me_ref, offset_ref, message_ref, own_ref, sine_ref, cosine_ref, *refs):
    *piece_refs, out_ref, sum_ref, part_ref = refs
    me = me_ref[0]
    inner = z.layers * z.tap_lanes
    tiles = 2 * 3 * inner // LANES
    count = z.width_p // LANES
    reach = (z.half + 1) * LANES
    sum_ref[...] = jnp.zeros_like(sum_ref)
    masks, middles = [], []
    for tile in range(tiles):
        lane = tile * LANES + lane_index((SUB, LANES))
        masks.append(row_masks(lane % inner // z.tap_lanes, lane // (3 * inner)))
        lane = tile * LANES + lane_index((z.angles, LANES))
        middles.append(lane // inner % 3 == 1)

    def brick_step(brick):
        taps = tap_rows(z, message_ref, brick)
        rise = 0.5 + 0.45 * sine_ref[...] * cosine_ref[brick]
        for side, weight in enumerate((taps * (1.0 - rise), taps * rise)):
            high, low = split(weight)
            for tile in range(tiles):
                at = ((brick * 2 + side) * tiles + tile) * z.angles
                part_ref[pl.ds(at, z.angles), :] = jnp.where(middles[tile], low, high)
        blocks = []
        for angle in range(z.angles):
            row = []
            for tile in range(tiles):
                at = (brick * 2 * tiles + tile) * z.angles + angle
                first = part_ref[pl.ds(at, SUB, 0), :]
                second = part_ref[pl.ds(at + tiles * z.angles, SUB, 0), :]
                same, above = masks[tile]
                row.append(jnp.where(same, first, jnp.where(above, second, 0.0)))
            blocks.append(jnp.concatenate(row, axis=1))
        left = jnp.concatenate(blocks, axis=0).astype(jnp.bfloat16)
        highs, lows = [], []
        for layer in range(z.layers):
            block = message_ref[
                brick, layer * z.slices : (layer + 1) * z.slices, : (2 * z.half + 1) * LANES
            ]
            for tap in range(z.taps):
                high, low = split(roll_left(block, z.taps - 1 - tap))
                highs.append(high)
                lows.append(low)
        high = jnp.concatenate(highs, axis=0).astype(jnp.bfloat16)
        low = jnp.concatenate(lows, axis=0).astype(jnp.bfloat16)
        right = []
        for begin in (0, z.half * LANES):
            part = high[:, begin : begin + reach]
            right += [part, part, low[:, begin : begin + reach]]
        product = jnp.dot(
            left, jnp.concatenate(right, axis=0), preferred_element_type=jnp.float32
        )
        for angle in range(z.angles):
            pieces = [
                product[angle * SUB : (angle + 1) * SUB, tile * LANES : (tile + 1) * LANES]
                for tile in range(z.half + 1)
            ]
            moved = shift_tiles(pieces, OFFMAX - offset_ref[angle, brick], z.half)
            for tile in range(z.half):
                rows = pl.ds((tile * z.angles + angle) * SUB, SUB)
                sum_ref[rows, :] = sum_ref[rows, :] + moved[tile]

    for_bricks(z, brick_step)
    lane = lane_index((z.angles, z.width_p))
    column = me * z.band - z.left + lane
    inside = (column >= 0) & (column < z.columns)
    for row in range(z.layers + 1):
        parts = []
        for tile in range(count):
            place, segment = tile % z.half, tile // z.half
            at = place * z.angles * SUB + segment * 4 + row
            parts.append(sum_ref[pl.ds(at, z.angles, SUB), :])
        total = -jnp.concatenate(parts, axis=1)
        if row < z.layers:
            window = own_ref[row]
            order = 0
            for away, first, last in z.pieces:
                if away == 0:
                    continue
                tail = piece_refs[order][row * z.angles : (row + 1) * z.angles]
                order += 1
                tail = jnp.concatenate(
                    [tail, jnp.zeros((z.angles, z.width_p - z.piece_p), jnp.float32)], axis=1
                )
                begin = first - away * z.band + z.left
                tail = roll_left(tail, -begin)
                here = (lane >= begin) & (lane < begin + last - first)
                window = jnp.where(here, tail, window)
            total = total + window
        out_ref[row] = jnp.where(inside, total, 0.0)


def adjoint_kernel(z, message_ref, sine_ref, cosine_ref, out_ref):
    inner = z.near_layers * z.tap_lanes
    tiles = -(-inner // LANES)
    masks = []
    for tile in range(tiles):
        layer = (tile * LANES + lane_index((SUB, LANES))) // z.tap_lanes
        row = lax.broadcasted_iota(jnp.int32, (SUB, LANES), 0)
        masks.append((row == layer, row == layer + 1))

    def brick_step(brick):
        taps = tap_rows(z, message_ref, brick)
        rise = 0.5 + 0.45 * sine_ref[...] * cosine_ref[brick]
        low, high = taps * (1.0 - rise), taps * rise
        columns = []
        for same, above in masks:
            blocks = []
            for angle in range(z.angles):
                first = jnp.broadcast_to(low[angle : angle + 1], (SUB, LANES))
                second = jnp.broadcast_to(high[angle : angle + 1], (SUB, LANES))
                blocks.append(jnp.where(same, first, jnp.where(above, second, 0.0)))
            columns.append(jnp.concatenate(blocks, axis=0).T)
        high, low = split(jnp.concatenate(columns, axis=0)[:inner])
        out_ref[brick] = jnp.concatenate([high, low, high], axis=1).astype(jnp.bfloat16)

    for_bricks(z, brick_step)


def finish_kernel(z, place_ref, offset_ref, own_ref, near_ref, far_ref, message_ref, near_volume_ref, far_volume_ref, weight_ref, *refs):
    *skip_refs, out_ref, row_ref, field_ref = refs
    height_of = place_ref[1]
    even = height_of % 2 == 0
    lower_pair = height_of % 4 < 2
    row_ref[...] = jnp.zeros_like(row_ref)
    below = [jnp.where(even, far_ref[row], near_ref[row]) for row in range(z.layers + 1)]
    above = [jnp.where(even, near_ref[row], far_ref[row]) for row in range(z.layers + 1)]
    above_two = jnp.where(lower_pair, skip_refs[0][...], skip_refs[-1][...])
    below_two = jnp.where(lower_pair, skip_refs[-1][...], skip_refs[0][...])
    below_two = jnp.where(height_of >= 2, below_two, 0.0)
    above_two = jnp.where(height_of + 2 < z.height, above_two, 0.0)
    own = [own_ref[row] for row in range(z.layers + 1)]
    own[0] = own[0] + jnp.where(height_of >= 1, below[z.layers], 0.0)
    below[0] = below[0] + below_two
    above_end = above_two + above[z.layers]
    above[0] = above[0] + own[z.layers]
    rows = below[: z.layers] + own[: z.layers] + above[: z.layers] + [above_end]
    for index, value in enumerate(rows):
        place = height_of * z.layers - z.margin + index
        value = jnp.where((place >= 0) & (place < z.height * z.layers), value, 0.0)
        for tile in range(z.width_p // LANES):
            row_ref[pl.ds(tile * z.angles * SUB + index, z.angles, SUB), :] = value[
                :, tile * LANES : (tile + 1) * LANES
            ]
    start = z.lead - z.lag
    count = z.field_p // LANES
    have = z.width_p // LANES

    def brick_step(brick):
        blocks = []
        for angle in range(z.angles):
            tiles = [
                row_ref[pl.ds((min(tile, have - 1) * z.angles + angle) * SUB, SUB), :]
                for tile in range(count + 1)
            ]
            moved = shift_tiles(tiles, OFFMAX + offset_ref[angle, brick], count)
            blocks.append(jnp.concatenate(moved, axis=1))
        high, low = split(jnp.concatenate(blocks, axis=0))
        high = high.astype(jnp.bfloat16)
        low = low.astype(jnp.bfloat16)
        product = jnp.dot(
            weight_ref[brick],
            jnp.concatenate([high, high, low], axis=0),
            preferred_element_type=jnp.float32,
        )
        for index in range(z.near_layers):
            update = None
            for tap in range(z.taps):
                begin = (index * z.taps + tap) * z.slices
                term = roll_left(product[begin : begin + z.slices], tap - z.lag)
                update = term if update is None else update + term
            layer = index % z.layers
            rows = pl.ds(layer * z.slices, z.slices)
            if z.margin <= index < z.margin + z.layers:
                voxels = message_ref[brick, rows, start : start + z.field_p]
            else:
                near, far = near_volume_ref[brick, rows, :], far_volume_ref[brick, rows, :]
                voxels = jnp.where(even == (index >= z.margin), near, far)
            field_ref[index, pl.ds(brick * z.slices, z.slices), :] = voxels + relax_step * update

    for_bricks(z, brick_step)

    shape = (z.total_slices, z.field_p)
    column = place_ref[0] * z.band - SWEEPS - z.lag + lane_index(shape)
    slice_at = lax.broadcasted_iota(jnp.int32, shape, 0)
    allow_x = (column >= 0) & (column + 1 < z.columns)
    allow_y = slice_at + 1 < z.total_slices
    not_first = slice_at > 0
    values = {index - z.margin: field_ref[index] for index in range(z.near_layers)}
    for sweep in range(SWEEPS):
        margin = SWEEPS - 1 - sweep
        later = {}
        before = None
        for layer in range(-margin - 1, z.layers + margin):
            here = values[layer]
            place = height_of * z.layers + layer
            allow_z = (place >= 0) & (place + 1 < z.height * z.layers)
            along_z = jnp.where(allow_z, values[layer + 1] - here, 0.0)
            along_y = jnp.where(allow_y, pltpu.roll(here, z.total_slices - 1, 0) - here, 0.0)
            along_x = jnp.where(allow_x, roll_left(here, 1) - here, 0.0)
            inverse = lax.rsqrt(
                tv_eps * tv_eps + along_z * along_z + along_y * along_y + along_x * along_x
            )
            normal_z = along_z * inverse
            if layer >= -margin:
                normal_y = along_y * inverse
                normal_x = along_x * inverse
                diverge = (
                    normal_z
                    - before
                    + normal_y
                    - jnp.where(not_first, pltpu.roll(normal_y, 1, 0), 0.0)
                    + normal_x
                    - pltpu.roll(normal_x, 1, 1)
                )
                later[layer] = here + tv_step * diverge
            before = normal_z
        values = later
    for layer in range(z.layers):
        result = roll_left(values[layer], SWEEPS + z.lag)
        for brick in range(z.depth):
            out_ref[brick, layer] = result[brick * z.slices : (brick + 1) * z.slices, : z.band]


def shifted(value, axis, by):
    count = lax.axis_size(axis)
    pairs = [(i, i + by) for i in range(count) if 0 <= i + by < count]
    return lax.ppermute(value, axis, pairs)


def swapped(value, first, step=1):
    depth, height = lax.axis_size("depth"), lax.axis_size("height")
    pairs = []
    for depth_at in range(depth):
        for height_at in range(height):
            partner = height_at + (step if (height_at - first) // step % 2 == 0 else -step)
            source = depth_at * height + height_at
            if 0 <= partner < height:
                pairs.append((source, depth_at * height + partner))
            elif depth_at ^ 1 < depth:
                pairs.append((source, (depth_at ^ 1) * height + height_at))
    return lax.ppermute(value, ("depth", "height"), pairs)


def call(kernel, z, shape, specs, scratch=(), dtype=jnp.float32, limit=16 << 20):
    return pl.pallas_call(
        lambda *refs: kernel(z, *refs),
        out_shape=jax.ShapeDtypeStruct(shape, dtype),
        in_specs=specs,
        out_specs=VMEM,
        scratch_shapes=list(scratch),
        compiler_params=pltpu.CompilerParams(vmem_limit_bytes=limit),
    )


def per_device(volume, measured, taps, band_offset, angle_index):
    z = Sizes(volume, taps, lax.axis_size("depth"), lax.axis_size("height"))
    depth_of = lax.axis_index("depth")
    height_of = lax.axis_index("height")
    place = jnp.stack([depth_of, height_of]).astype(jnp.int32)

    pieces = []
    for away, first, last in z.pieces:
        if away == 0:
            continue
        piece = jnp.transpose(measured[:, :, first:last], (1, 0, 2))
        piece = jnp.pad(piece, ((0, 0), (0, 0), (0, z.piece_p - (last - first))))
        piece = piece.reshape(z.layers * z.angles, z.piece_p)
        pieces.append(shifted(piece, "depth", away))
    own = jnp.pad(
        jnp.transpose(measured, (1, 0, 2)),
        ((0, 0), (0, 0), (z.left, z.width_p - z.left - z.band)),
    )
    angle_value = 2.0 * math.pi / N_VIEWS * angle_index.astype(jnp.float32)
    sine = jnp.broadcast_to(jnp.sin(angle_value)[:, None], (z.angles, LANES))
    slice_at = (
        jnp.arange(z.depth, dtype=jnp.int32)[:, None] * z.slices
        + jnp.arange(LANES, dtype=jnp.int32)[None, :] % z.slices
    )
    cosine = jnp.cos(math.pi / z.total_slices * (slice_at.astype(jnp.float32) + 0.5))[:, None, :]

    message = call(
        pack_kernel, z, (z.depth, z.rows, z.message), [VMEM, VMEM], limit=None
    )(
        volume.reshape(z.rows, z.columns),
        jnp.transpose(taps, (0, 2, 1)).reshape(z.tap_lanes, z.angles),
    )
    message = lax.all_to_all(message, "depth", 0, 0)
    start = z.lead - z.lag
    voxels = message[:, :, start : start + z.field_p]
    volume_far = swapped(voxels, 1)
    volume_near = swapped(voxels, 0)
    tiles = 2 * 3 * z.layers * z.tap_lanes // LANES
    partial = call(
        project_kernel,
        z,
        (z.layers + 1, z.angles, z.width_p),
        [SMEM, SMEM, VMEM, VMEM, VMEM, VMEM] + [VMEM] * len(pieces),
        [
            pltpu.VMEM((z.half * z.angles * SUB, LANES), jnp.float32),
            pltpu.VMEM((z.depth * 2 * tiles * z.angles + SUB, LANES), jnp.float32),
        ],
    )(place, band_offset, message, own, sine, cosine, *pieces)
    lower_pair = height_of % 4 < 2
    upward, downward = partial[z.layers], partial[0]
    far = swapped(partial, 1)
    skips = [swapped(jnp.where(lower_pair, upward, downward), 0, 2)]
    if z.height > 4:
        skips.append(swapped(jnp.where(lower_pair, downward, upward), 2, 2))
    near = swapped(partial, 0)
    weight = call(
        adjoint_kernel,
        z,
        (z.depth, z.near_layers * z.tap_lanes, 3 * z.angles * SUB),
        [VMEM, VMEM, VMEM],
        dtype=jnp.bfloat16,
    )(message, sine, cosine)
    bands = call(
        finish_kernel,
        z,
        (z.depth, z.layers, z.slices, z.band),
        [SMEM, SMEM] + [VMEM] * (7 + len(skips)),
        [
            pltpu.VMEM((z.width_p // LANES * z.angles * SUB, LANES), jnp.float32),
            pltpu.VMEM((z.near_layers, z.total_slices, z.field_p), jnp.float32),
        ],
    )(
        place, band_offset, partial, near, far, message, volume_near, volume_far, weight, *skips
    )
    bands = lax.all_to_all(bands, "depth", 0, 0)
    return jnp.transpose(bands, (1, 2, 0, 3)).reshape(volume.shape)


def solution(mesh):
    in_specs = (
        P("height", "depth", None),
        P(None, "height", "depth"),
        P(None, None, "depth"),
        P(),
        P(),
    )
    out_specs = P("height", "depth", None)

    return jax.shard_map(
        per_device, mesh=mesh, in_specs=in_specs, out_specs=out_specs, check_vma=False
    )
```
